32 devices in a mesh: wide: 16 (over z, y, core), narrow: 2 (over x).
Axes of the slice: x: 2, y: 2, z: 4, core: 2. Of those that a mesh axis runs over, the one named last changes fastest.
Arguments:
- tokens: bfloat16 [32, 256, 1120], P(('wide', 'narrow')), may hold values from -6 to 6
- lengths: int32 [32], P(('wide', 'narrow')), may hold values from 128 to 256
- dropped: int32 [32], P(('wide', 'narrow')), may hold values from 0 to 4
- cotangent: bfloat16 [32, 256, 1120], P(('wide', 'narrow')), may hold values from -6 to 6
- first_gain: bfloat16 [1120], P('narrow'), may hold values from 0.5 to 1.5
- first_shift: bfloat16 [1120], P('narrow'), may hold values from -1.5 to 1.5
- qkv_weight: bfloat16 [1120, 3360], P('narrow'), may hold values from -0.1875 to 0.1875
- query_bias: bfloat16 [1120], P('narrow'), may hold values from -2 to 2
- value_bias: bfloat16 [1120], P('narrow'), may hold values from -2 to 2
- out_weight: bfloat16 [1120, 1120], P('narrow'), may hold values from -1.5 to 1.5
- out_bias: bfloat16 [1120], P('narrow'), may hold values from -1.5 to 1.5
- second_gain: bfloat16 [1120], P('narrow'), may hold values from 0.5 to 1.5
- second_shift: bfloat16 [1120], P('narrow'), may hold values from -1.5 to 1.5
- up_weight: bfloat16 [1120, 4480], P('narrow'), may hold values from -0.1875 to 0.1875
- up_bias: bfloat16 [4480], P('narrow'), may hold values from -2 to 2
- down_weight: bfloat16 [4480, 1120], P('narrow'), may hold values from -0.1875 to 0.1875
- down_bias: bfloat16 [1120], P('narrow'), may hold values from -1.5 to 1.5
Outputs:
- output: bfloat16 [32, 256, 1120], P(('wide', 'narrow'))
- grad_tokens: float32 [32, 256, 1120], P(('wide', 'narrow'))
- grad_first_gain: float32 [1120], P('narrow')
- grad_first_shift: float32 [1120], P('narrow')
- grad_qkv_weight: float32 [1120, 3360], P('narrow', 'wide')
- grad_query_bias: float32 [1120], P('narrow')
- grad_value_bias: float32 [1120], P('narrow')
- grad_out_weight: float32 [1120, 1120], P('narrow', 'wide')
- grad_out_bias: float32 [1120], P('narrow')
- grad_second_gain: float32 [1120], P('narrow')
- grad_second_shift: float32 [1120], P('narrow')
- grad_up_weight: float32 [1120, 4480], P('narrow', 'wide')
- grad_up_bias: float32 [4480], P('narrow')
- grad_down_weight: float32 [4480, 1120], P('narrow', 'wide')
- grad_down_bias: float32 [1120], P('narrow')
The draws below stay inside these ranges and needn't reach their ends.
All inputs are finite; a program needn't handle non-finite values.
Results may differ from the reference program's by a relative error of at most 0.018.
Values may be sent and summed in bfloat16 or wider, within the bound.
A program may use at most 192 MiB of HBM per device.

```python
import jax
import jax.numpy as jnp
from jax import lax

D = 1120
HEADS = 20
HEAD = 56
FF = 4480
LEN = 256
SEQS = 32


def plant(values, stream_key, least, high):
    longest = values.shape.index(max(values.shape))
    spots = []
    for shift in (0, 1):
        where = [jax.random.randint(jax.random.fold_in(stream_key, axis), (), 0, length) for axis, length in enumerate(values.shape)]
        where[longest] = (where[longest] + shift) % values.shape[longest]
        spots.append(tuple(where))
    return values.at[spots[0]].set(least).at[spots[1]].set(high)


def steps_of(own_key, shape, pieces, smallest, high):
    factor_of = 1.0
    for dim, blocks in pieces:
        heights = jax.random.uniform(jax.random.fold_in(jax.random.fold_in(own_key, 6), dim), (blocks,), jnp.float32, smallest / len(pieces), high / len(pieces))
        factor_of = factor_of * jnp.repeat(jnp.exp(heights), shape[dim] // blocks).reshape((-1,) + (1,) * (len(shape) - 1 - dim))
    return factor_of


def gaussian(rng, dims, width, most, pieces=(), kind=jnp.bfloat16):
    drawn = jax.random.normal(rng, dims, jnp.float32) * width
    if len(pieces) > 0:
        drawn = steps_of(rng, dims, pieces, -0.22, 0.18) * drawn
    return jnp.clip(drawn, min=-most, max=most).astype(kind)


def setup_inputs(seed: int = 0) -> dict:
    seeds = jax.random.split(jax.random.key(seed), 18)
    tokens = gaussian(seeds[0], (SEQS, LEN, D), 1.0, 6.0, ((0, 32),))
    lengths = plant(jax.random.randint(seeds[1], (SEQS,), LEN // 2, LEN + 1), jax.random.fold_in(seeds[1], 1), LEN // 2, LEN).astype(jnp.int32)
    dropped = plant(jax.random.randint(seeds[2], (SEQS,), 0, 5), jax.random.fold_in(seeds[2], 1), 0, 4).astype(jnp.int32)
    cotangent = gaussian(seeds[3], (SEQS, LEN, D), 1.0, 6.0, ((0, 32),))
    first_gain = jnp.clip(1.0 + 0.1 * jax.random.normal(seeds[4], (D,), jnp.float32), 0.5, 1.5).astype(jnp.bfloat16)
    first_shift = gaussian(seeds[5], (D,), 0.3, 1.5, ((0, 2),))
    qkv_weight = gaussian(seeds[6], (D, 3 * D), D ** -0.5, 0.1875, ((0, 2),))
    query_bias = gaussian(seeds[7], (D,), 0.4, 2.0, ((0, 2),))
    value_bias = gaussian(seeds[8], (D,), 0.4, 2.0, ((0, 2),))
    out_weight = gaussian(seeds[9], (D, D), (max(4 * D // LEN, 1)) ** -0.5, 1.5, ((0, 2),))
    out_bias = gaussian(seeds[10], (D,), 0.3, 1.5, ((0, 2),))
    second_gain = jnp.clip(1.0 + 0.1 * jax.random.normal(seeds[11], (D,), jnp.float32), 0.5, 1.5).astype(jnp.bfloat16)
    second_shift = gaussian(seeds[12], (D,), 0.3, 1.5, ((0, 2),))
    up_weight = gaussian(seeds[13], (D, FF), D ** -0.5, 0.1875, ((0, 2),))
    up_bias = gaussian(seeds[14], (FF,), 0.4, 2.0, ((0, 2),))
    down_weight = gaussian(seeds[15], (FF, D), (FF // 4) ** -0.5, 0.1875, ((0, 2),))
    down_bias = gaussian(seeds[16], (D,), 0.3, 1.5, ((0, 2),))
    return dict(tokens=tokens, lengths=lengths, dropped=dropped, cotangent=cotangent, first_gain=first_gain, first_shift=first_shift, qkv_weight=qkv_weight, query_bias=query_bias, value_bias=value_bias, out_weight=out_weight, out_bias=out_bias, second_gain=second_gain, second_shift=second_shift, up_weight=up_weight, up_bias=up_bias, down_weight=down_weight, down_bias=down_bias)


@jax.custom_vjp
def low(v):
    return lax.optimization_barrier(v.astype(jnp.bfloat16)).astype(jnp.float32)

@jax.custom_vjp
def low_back(v):
    return v

def low_keep(v):
    return (low(v), None)

def low_pass(kept, grad):
    return (grad,)

def back_keep(v):
    return (v, None)

def back_low(kept, grad):
    return (low(grad),)
low.defvjp(low_keep, low_pass)
low_back.defvjp(back_keep, back_low)
epsilon = 1e-05

def normed(values, gain, shift):
    center = values - lax.optimization_barrier(jnp.mean(values, axis=-1, keepdims=True))
    spread = lax.optimization_barrier(jnp.mean(center * center, axis=-1, keepdims=True))
    return center * lax.rsqrt(spread + epsilon) * gain + shift

def matmul(left, right):
    return jnp.dot(left, right, precision=lax.Precision.HIGHEST)

def key_mask(length, drop):
    places = jnp.arange(LEN, dtype=jnp.int32)
    live = (places < length) & ((places < 1) | (places > drop))
    return (places[None, :] <= places[:, None]) & (live[None, :] | (places[None, :] == places[:, None]))

def layer(inputs, params, mask):
    first_gain, first_shift, qkv_weight, query_bias, value_bias, out_weight, out_bias, second_gain, second_shift, up_weight, up_bias, down_weight, down_bias = params
    first = low(normed(inputs, first_gain, first_shift))
    mixed = matmul(first, qkv_weight)
    query = low(low_back(mixed[:, :D] + query_bias)).reshape(LEN, HEADS, HEAD)
    keys = low(low_back(mixed[:, D:2 * D])).reshape(LEN, HEADS, HEAD)
    values = low(low_back(mixed[:, 2 * D:] + value_bias)).reshape(LEN, HEADS, HEAD)
    scores = jnp.einsum('qhe,khe->hqk', query, keys, precision=lax.Precision.HIGHEST) * HEAD ** (-0.5)
    scores = jnp.where(mask[None], low_back(scores), -jnp.inf)
    probs = low(jax.nn.softmax(scores, axis=-1))
    attended = jnp.einsum('hqk,khe->qhe', probs, values, precision=lax.Precision.HIGHEST).reshape(LEN, D)
    attended = low(low_back(attended))
    middle = inputs + low_back(matmul(attended, out_weight) + out_bias)
    second = low(normed(middle, second_gain, second_shift))
    hidden = low_back(matmul(second, up_weight) + up_bias)
    active = low(jax.nn.gelu(hidden, approximate=True))
    return middle + (matmul(active, down_weight) + down_bias)

def reference(tokens, lengths, dropped, cotangent, first_gain, first_shift, qkv_weight, query_bias, value_bias, out_weight, out_bias, second_gain, second_shift, up_weight, up_bias, down_weight, down_bias):
    params = tuple((w.astype(jnp.float32) for w in (first_gain, first_shift, qkv_weight, query_bias, value_bias, out_weight, out_bias, second_gain, second_shift, up_weight, up_bias, down_weight, down_bias)))

    def one_sentence(totals, item):
        sentence, length, drop, grad_out = item
        mask = key_mask(length, drop)
        result, pull = jax.vjp(lambda xs, ps: layer(xs, ps, mask), sentence.astype(jnp.float32), params)
        grad_input, grad_params = pull(grad_out.astype(jnp.float32))
        totals = jax.tree.map(lambda a, b: a + b, totals, grad_params)
        return (totals, (result.astype(jnp.bfloat16), grad_input))
    zeros = tuple((jnp.zeros(p.shape, jnp.float32) for p in params))
    totals, (output, grad_tokens) = lax.scan(one_sentence, zeros, (tokens, lengths, dropped, cotangent))
    return (output, grad_tokens, totals[0], totals[1], totals[2], totals[3], totals[4], totals[5], totals[6], totals[7], totals[8], totals[9], totals[10], totals[11], totals[12])
```

```python
import jax
import jax.numpy as jnp
from jax import lax
from jax.sharding import PartitionSpec as P

HEAD = 56
epsilon = 1e-05
head_groups = 4
AXES = ("wide", "narrow")
f32 = jnp.float32
bf16 = jnp.bfloat16


def dot(left, right):
    return jnp.dot(left, right, preferred_element_type=f32)


def tdot(left, right):
    return lax.dot_general(left, right, (((0,), (0,)), ((), ())), preferred_element_type=f32)


def dot_t(left, right):
    return lax.dot_general(left, right, (((1,), (1,)), ((), ())), preferred_element_type=f32)


def normed(values, gain, shift):
    center = values - jnp.mean(values, axis=-1, keepdims=True)
    spread = jnp.mean(center * center, axis=-1, keepdims=True)
    return center * lax.rsqrt(spread + epsilon) * gain + shift


def split_heads(matrix):
    rows = matrix.shape[0]
    return matrix.reshape(rows, head_groups, -1, HEAD).transpose(1, 0, 2, 3)


def join_heads(blocks):
    return blocks.transpose(1, 0, 2, 3).reshape(blocks.shape[1], -1)


def key_mask(length, drop, rows):
    places = jnp.arange(rows, dtype=jnp.int32)
    live = (places < length) & ((places < 1) | (places > drop))
    return (places[None, :] <= places[:, None]) & (
        live[None, :] | (places[None, :] == places[:, None])
    )


def scores_of(query, keys, mask):
    raw = jnp.einsum("qhe,khe->hqk", query, keys, preferred_element_type=f32) * HEAD ** (-0.5)
    return jnp.where(mask[None], raw, -jnp.inf)


def attention(query, keys, values, mask):
    def attend(group):
        scores = scores_of(group[0], group[1], mask)
        top = jnp.max(scores, axis=-1, keepdims=True)
        expos = jnp.exp(scores - top)
        total = jnp.sum(expos, axis=-1, keepdims=True)
        probs = (expos / total).astype(bf16)
        heads_out = jnp.einsum("hqk,khe->qhe", probs, group[2], preferred_element_type=f32)
        return (heads_out.astype(bf16), top + jnp.log(total))

    heads_out, logsum = lax.map(
        attend, (split_heads(query), split_heads(keys), split_heads(values))
    )
    return join_heads(heads_out), logsum


def attention_back(query, keys, values, logsum, d_attended, mask):
    def attend_back(group):
        q_part, k_part, v_part, lse_part, do_part = group
        scores = scores_of(q_part, k_part, mask)
        probs = jnp.exp(scores - lse_part)
        rounded = probs.astype(bf16)
        d_v = jnp.einsum("hqk,qhe->khe", rounded, do_part, preferred_element_type=f32)
        d_probs = jnp.einsum("qhe,khe->hqk", do_part, v_part, preferred_element_type=f32)
        inner = jnp.sum(d_probs * probs, axis=-1, keepdims=True)
        d_scores = (probs * (d_probs - inner)).astype(bf16)
        d_q = jnp.einsum("hqk,khe->qhe", d_scores, k_part, preferred_element_type=f32)
        d_k = jnp.einsum("hqk,qhe->khe", d_scores, q_part, preferred_element_type=f32)
        d_q = d_q * HEAD ** (-0.5)
        d_k = d_k * HEAD ** (-0.5)
        return (d_q.astype(bf16), d_k.astype(bf16), d_v.astype(bf16))

    d_qs, d_ks, d_vs = lax.map(
        attend_back,
        (
            split_heads(query),
            split_heads(keys),
            split_heads(values),
            logsum,
            split_heads(d_attended),
        ),
    )
    return join_heads(d_qs), join_heads(d_ks), join_heads(d_vs)


class Links:
    def __init__(self):
        self.count = lax.axis_size("narrow")
        self.wide = lax.axis_size("wide")
        self.x = lax.axis_index("narrow")
        spot = lax.axis_index("wide")
        self.core = spot % 2
        self.y = (spot // 2) % 2
        self.z = spot // 4
        self.depth = self.wide // 4
        self.direct = self.count == 2 and self.wide == 16

    def table(self, move):
        pairs = []
        for i in range(self.count * self.wide):
            x = i % self.count
            spot = i // self.count
            to = move(x, (spot // 2) % 2, spot // 4, spot % 2)
            if to is not None:
                pairs.append((i, ((to[2] * 2 + to[1]) * 2 + to[3]) * self.count + to[0]))
        return pairs

    def send(self, value, move):
        return lax.ppermute(value, AXES, self.table(move))

    def over_x(self, value):
        return self.send(value, lambda x, y, z, c: (1 - x, y, z, c))

    def over_y(self, value):
        return self.send(value, lambda x, y, z, c: (x, 1 - y, z, c))

    def over_core(self, value):
        return self.send(value, lambda x, y, z, c: (x, y, z, 1 - c))


def pick(which, zero, one):
    return jnp.where(which == 0, zero, one)


def gather_other(links, shard):
    rows, columns = shard.shape
    tiles = rows // 8
    span = -(-tiles // 4)
    starts = [tiles * k // 4 for k in range(4)]
    view = shard.reshape(tiles, 8, columns)
    start_of = jnp.array(starts, jnp.int32)
    mine = links.y * 2 + links.core

    def at(y, core):
        return start_of[y * 2 + core]

    piece = lax.dynamic_slice_in_dim(view, start_of[mine], span, 0)
    first = links.over_x(piece)
    second = links.over_y(first)
    third = links.over_core(first)
    fourth = links.over_core(second)
    whole = jnp.zeros((tiles, 8, columns), shard.dtype)
    y, core = links.y, links.core
    for value, spot in (
        (first, at(y, core)),
        (second, at(1 - y, core)),
        (third, at(y, 1 - core)),
        (fourth, at(1 - y, 1 - core)),
    ):
        whole = lax.dynamic_update_slice_in_dim(whole, value, spot, 0)
    return whole.reshape(rows, columns)


class Weight:
    def __init__(self, links, shard):
        self.links = links
        self.own = shard
        if links.direct:
            self.other = gather_other(links, shard)
        else:
            self.full = lax.all_gather(shard, "narrow", axis=0, tiled=True)

    def apply(self, left):
        if not self.links.direct:
            return dot(left, self.full)
        x = self.links.x
        half = left.shape[1] // 2
        mine = pick(x, left[:, :half], left[:, half:])
        theirs = pick(x, left[:, half:], left[:, :half])
        return dot(mine, self.own) + dot(theirs, self.other)

    def apply_t(self, left):
        if not self.links.direct:
            return dot_t(left, self.full)
        x = self.links.x
        mine = dot_t(left, self.own)
        theirs = dot_t(left, self.other)
        return jnp.concatenate([pick(x, mine, theirs), pick(x, theirs, mine)], axis=1)


def weight_grad(links, left, right):
    if not links.direct:
        grad = tdot(left, right).astype(bf16)
        grad = lax.psum_scatter(grad, "narrow", scatter_dimension=0, tiled=True)
        return lax.psum_scatter(grad, "wide", scatter_dimension=1, tiled=True).astype(f32)
    x, y, z, core = links.x, links.y, links.z, links.core
    rows, columns = left.shape[1], right.shape[1]
    half = rows // 2
    unit = columns // 8
    right_own = pick(core, right[:, : columns // 2], right[:, columns // 2 :])
    right_away = pick(core, right[:, columns // 2 :], right[:, : columns // 2])
    right_all = jnp.concatenate([right_own, links.over_core(right_away)], axis=0)
    left_all = jnp.concatenate([left, links.over_core(left)], axis=0)
    left_own = pick(x, left_all[:, :half], left_all[:, half:])
    left_away = pick(x, left_all[:, half:], left_all[:, :half])
    cut = [right_all[:, k * unit : (k + 1) * unit] for k in range(4)]
    near = [pick(y, cut[0], cut[1]), pick(y, cut[2], cut[3])]
    far = [pick(y, cut[1], cut[0]), pick(y, cut[3], cut[2])]

    def both(one, two):
        return jnp.stack([one.astype(bf16), two.astype(bf16)])

    got_x = links.over_x(both(tdot(far[0], left_away), tdot(near[0], left_away)))
    got_y = links.over_y(both(tdot(far[1], left_away), tdot(far[1], left_own)))
    sum_far = tdot(far[0], left_own) + got_x[0].astype(f32)
    even = tdot(near[0], left_own) + got_x[1].astype(f32)
    sum_away = tdot(near[1], left_away) + got_y[0].astype(f32)
    odd = tdot(near[1], left_own) + got_y[1].astype(f32)
    even = even + links.over_y(sum_far.astype(bf16)).astype(f32)
    odd = odd + links.over_x(sum_away.astype(bf16)).astype(f32)
    low = z % 2 == 0
    even_b, odd_b = even.astype(bf16), odd.astype(bf16)
    same = jnp.where(low, odd_b, even_b)
    straight = jnp.where(low, even_b, odd_b)
    got_1 = links.send(same, lambda x, y, z, c: (x, y, z ^ 1, c) if z // 2 == c else None)
    got_2 = links.send(straight, lambda x, y, z, c: (x, y, z ^ 2, c) if z // 2 != c else None)
    got_3 = links.send(same, lambda x, y, z, c: (x, y, z ^ 3, c) if z // 2 != c else None)
    total = jnp.where(low, even, odd)
    total = total + got_1.astype(f32) + got_2.astype(f32) + got_3.astype(f32)
    part = unit // 2
    zero_part, one_part = total[:part], total[part:]
    got = links.send(
        pick(core, one_part, zero_part),
        lambda x, y, z, c: (x, y, z, 1 - c) if z // 2 == c else None,
    )
    result = jnp.where(z // 2 == core, pick(core, zero_part, one_part), got)
    return result.T


def gather_vectors(links, vectors):
    lengths = [v.shape[0] for v in vectors]
    if not links.direct:
        return [lax.all_gather(v, "narrow", axis=0, tiled=True).astype(f32) for v in vectors]
    packed = jnp.concatenate(vectors)
    other = links.over_x(packed)
    full = []
    at = 0
    for length in lengths:
        mine, theirs = packed[at : at + length], other[at : at + length]
        joined = jnp.concatenate([pick(links.x, mine, theirs), pick(links.x, theirs, mine)])
        full.append(joined.astype(f32))
        at += length
    return full


def vector_grads(links, sums):
    lengths = [v.shape[0] for v in sums]
    total = lax.psum(jnp.concatenate(sums), AXES)
    parts = []
    at = 0
    for length in lengths:
        own = length // links.count
        parts.append(lax.dynamic_slice_in_dim(total, at + links.x * own, own, 0))
        at += length
    return parts


def local(
    tokens,
    lengths,
    dropped,
    cotangent,
    first_gain,
    first_shift,
    qkv_weight,
    query_bias,
    value_bias,
    out_weight,
    out_bias,
    second_gain,
    second_shift,
    up_weight,
    up_bias,
    down_weight,
    down_bias,
):
    links = Links()
    rows, width = tokens.shape[1:]
    mask = key_mask(lengths[0], dropped[0], rows)
    inputs = tokens[0].astype(f32)
    grad_out = cotangent[0]
    (gain1, shift1, q_bias, v_bias, o_bias, gain2, shift2, d_bias, u_bias) = gather_vectors(
        links,
        [
            first_gain,
            first_shift,
            query_bias,
            value_bias,
            out_bias,
            second_gain,
            second_shift,
            down_bias,
            up_bias,
        ],
    )
    w_qkv = Weight(links, qkv_weight)
    w_out = Weight(links, out_weight)
    w_up = Weight(links, up_weight)
    w_down = Weight(links, down_weight)

    first = normed(inputs, gain1, shift1).astype(bf16)
    mixed = w_qkv.apply(first)
    query = (mixed[:, :width] + q_bias).astype(bf16)
    keys = mixed[:, width : 2 * width].astype(bf16)
    values = (mixed[:, 2 * width :] + v_bias).astype(bf16)
    attended, logsum = attention(query, keys, values, mask)
    middle = inputs + (w_out.apply(attended) + o_bias)
    second = normed(middle, gain2, shift2).astype(bf16)
    hidden = w_up.apply(second) + u_bias
    active = jax.nn.gelu(hidden, approximate=True).astype(bf16)
    g_down = weight_grad(links, active, grad_out)
    result = middle + (w_down.apply(active) + d_bias)
    output = result.astype(bf16)[None]

    d_active = w_down.apply_t(grad_out)
    unused, gelu_pull = jax.vjp(lambda v: jax.nn.gelu(v, approximate=True), hidden)
    d_hidden = gelu_pull(d_active)[0].astype(bf16)
    g_up = weight_grad(links, second, d_hidden)
    d_second = w_up.apply_t(d_hidden)
    unused, norm_pull = jax.vjp(normed, middle, gain2, shift2)
    d_middle, d_gain2, d_shift2 = norm_pull(d_second)
    d_middle = d_middle + grad_out.astype(f32)
    d_branch = d_middle.astype(bf16)
    g_out = weight_grad(links, attended, d_branch)
    d_attended = w_out.apply_t(d_branch).astype(bf16)
    d_query, d_keys, d_values = attention_back(query, keys, values, logsum, d_attended, mask)
    d_mixed = jnp.concatenate([d_query, d_keys, d_values], axis=1)
    g_qkv = weight_grad(links, first, d_mixed)
    d_first = w_qkv.apply_t(d_mixed)
    unused, first_pull = jax.vjp(normed, inputs, gain1, shift1)
    d_inputs, d_gain1, d_shift1 = first_pull(d_first)
    grad_tokens = (d_middle + d_inputs)[None]

    def column_sum(values):
        return jnp.sum(values.astype(f32), axis=0)

    v_gain1, v_shift1, v_q, v_v, v_o, v_gain2, v_shift2, v_up, v_down = vector_grads(
        links,
        [
            d_gain1,
            d_shift1,
            column_sum(d_query),
            column_sum(d_values),
            column_sum(d_branch),
            d_gain2,
            d_shift2,
            column_sum(d_hidden),
            column_sum(grad_out),
        ],
    )
    return (
        output,
        grad_tokens,
        v_gain1,
        v_shift1,
        g_qkv,
        v_q,
        v_v,
        g_out,
        v_o,
        v_gain2,
        v_shift2,
        g_up,
        v_up,
        g_down,
        v_down,
    )


def solution(mesh):
    batch = P(AXES, None, None)
    vector = P("narrow")
    matrix = P("narrow", None)
    return jax.shard_map(
        local,
        mesh=mesh,
        in_specs=(
            batch,
            P(AXES),
            P(AXES),
            batch,
            vector,
            vector,
            matrix,
            vector,
            vector,
            matrix,
            vector,
            vector,
            vector,
            matrix,
            vector,
            matrix,
            vector,
        ),
        out_specs=(
            batch,
            batch,
            vector,
            vector,
            P("narrow", "wide"),
            vector,
            vector,
            P("narrow", "wide"),
            vector,
            vector,
            vector,
            P("narrow", "wide"),
            vector,
            P("narrow", "wide"),
            vector,
        ),
        check_vma=False,
    )
```

```python
import functools

import jax
import jax.numpy as jnp
from jax import lax
from jax.experimental import pallas as pl
from jax.experimental.pallas import tpu as pltpu
from jax.sharding import PartitionSpec as P

HEAD = 56
epsilon = 1e-05
head_groups = 4
AXES = ("wide", "narrow")
f32 = jnp.float32
bf16 = jnp.bfloat16


def dot(left, right):
    return jnp.dot(left, right, preferred_element_type=f32)


def tdot(left, right):
    return lax.dot_general(left, right, (((0,), (0,)), ((), ())), preferred_element_type=f32)


def dot_t(left, right):
    return lax.dot_general(left, right, (((1,), (1,)), ((), ())), preferred_element_type=f32)


def normed(values, gain, shift):
    center = values - jnp.mean(values, axis=-1, keepdims=True)
    spread = jnp.mean(center * center, axis=-1, keepdims=True)
    return center * lax.rsqrt(spread + epsilon) * gain + shift


def split_heads(matrix):
    rows = matrix.shape[0]
    return matrix.reshape(rows, head_groups, -1, HEAD).transpose(1, 0, 2, 3)


def join_heads(blocks):
    return blocks.transpose(1, 0, 2, 3).reshape(blocks.shape[1], -1)


def key_mask(length, drop, rows):
    places = jnp.arange(rows, dtype=jnp.int32)
    live = (places < length) & ((places < 1) | (places > drop))
    return (places[None, :] <= places[:, None]) & (
        live[None, :] | (places[None, :] == places[:, None])
    )


def scores_of(query, keys, mask):
    raw = jnp.einsum("qhe,khe->hqk", query, keys, preferred_element_type=f32) * HEAD ** (-0.5)
    return jnp.where(mask[None], raw, -jnp.inf)


def attention(query, keys, values, mask):
    def attend(group):
        scores = scores_of(group[0], group[1], mask)
        top = jnp.max(scores, axis=-1, keepdims=True)
        expos = jnp.exp(scores - top)
        total = jnp.sum(expos, axis=-1, keepdims=True)
        probs = (expos / total).astype(bf16)
        heads_out = jnp.einsum("hqk,khe->qhe", probs, group[2], preferred_element_type=f32)
        return (heads_out.astype(bf16), top + jnp.log(total))

    heads_out, logsum = lax.map(
        attend, (split_heads(query), split_heads(keys), split_heads(values))
    )
    return join_heads(heads_out), logsum


def attention_back(query, keys, values, logsum, d_attended, mask):
    def attend_back(group):
        q_part, k_part, v_part, lse_part, do_part = group
        scores = scores_of(q_part, k_part, mask)
        probs = jnp.exp(scores - lse_part)
        rounded = probs.astype(bf16)
        d_v = jnp.einsum("hqk,qhe->khe", rounded, do_part, preferred_element_type=f32)
        d_probs = jnp.einsum("qhe,khe->hqk", do_part, v_part, preferred_element_type=f32)
        inner = jnp.sum(d_probs * probs, axis=-1, keepdims=True)
        d_scores = (probs * (d_probs - inner)).astype(bf16)
        d_q = jnp.einsum("hqk,khe->qhe", d_scores, k_part, preferred_element_type=f32)
        d_k = jnp.einsum("hqk,qhe->khe", d_scores, q_part, preferred_element_type=f32)
        d_q = d_q * HEAD ** (-0.5)
        d_k = d_k * HEAD ** (-0.5)
        return (d_q.astype(bf16), d_k.astype(bf16), d_v.astype(bf16))

    d_qs, d_ks, d_vs = lax.map(
        attend_back,
        (
            split_heads(query),
            split_heads(keys),
            split_heads(values),
            logsum,
            split_heads(d_attended),
        ),
    )
    return join_heads(d_qs), join_heads(d_ks), join_heads(d_vs)


class Links:
    def __init__(self):
        self.count = lax.axis_size("narrow")
        self.wide = lax.axis_size("wide")
        self.x = lax.axis_index("narrow")
        spot = lax.axis_index("wide")
        self.core = spot % 2
        self.y = (spot // 2) % 2
        self.z = spot // 4
        self.depth = self.wide // 4
        self.direct = self.count == 2 and self.wide == 16

    def table(self, move):
        pairs = []
        for i in range(self.count * self.wide):
            x = i % self.count
            spot = i // self.count
            to = move(x, (spot // 2) % 2, spot // 4, spot % 2)
            if to is not None:
                pairs.append((i, ((to[2] * 2 + to[1]) * 2 + to[3]) * self.count + to[0]))
        return pairs

    def send(self, value, move):
        return lax.ppermute(value, AXES, self.table(move))

    def over_x(self, value):
        return self.send(value, lambda x, y, z, c: (1 - x, y, z, c))

    def over_y(self, value):
        return self.send(value, lambda x, y, z, c: (x, 1 - y, z, c))

    def over_core(self, value):
        return self.send(value, lambda x, y, z, c: (x, y, z, 1 - c))


def pick(which, zero, one):
    return jnp.where(which == 0, zero, one)


def gather_other(links, shard):
    rows, columns = shard.shape
    tiles = rows // 8
    span = -(-tiles // 4)
    starts = [tiles * k // 4 for k in range(4)]
    view = shard.reshape(tiles, 8, columns)
    start_of = jnp.array(starts, jnp.int32)
    mine = links.y * 2 + links.core

    def at(y, core):
        return start_of[y * 2 + core]

    piece = lax.dynamic_slice_in_dim(view, start_of[mine], span, 0)
    first = links.over_x(piece)
    second = links.over_y(first)
    third = links.over_core(first)
    fourth = links.over_core(second)
    whole = jnp.zeros((tiles, 8, columns), shard.dtype)
    y, core = links.y, links.core
    for value, spot in (
        (first, at(y, core)),
        (second, at(1 - y, core)),
        (third, at(y, 1 - core)),
        (fourth, at(1 - y, 1 - core)),
    ):
        whole = lax.dynamic_update_slice_in_dim(whole, value, spot, 0)
    return whole.reshape(rows, columns)


class Weight:
    def __init__(self, links, shard):
        self.links = links
        self.own = shard
        if links.direct:
            self.other = gather_other(links, shard)
        else:
            self.full = lax.all_gather(shard, "narrow", axis=0, tiled=True)

    def apply(self, left):
        if not self.links.direct:
            return dot(left, self.full)
        x = self.links.x
        half = left.shape[1] // 2
        mine = pick(x, left[:, :half], left[:, half:])
        theirs = pick(x, left[:, half:], left[:, :half])
        return dot(mine, self.own) + dot(theirs, self.other)

    def apply_t(self, left):
        if not self.links.direct:
            return dot_t(left, self.full)
        x = self.links.x
        mine = dot_t(left, self.own)
        theirs = dot_t(left, self.other)
        return jnp.concatenate([pick(x, mine, theirs), pick(x, theirs, mine)], axis=1)


MESH = pl.DeviceIdType.MESH


def generic_grad(links, left, right):
    grad = tdot(left, right).astype(bf16)
    grad = lax.psum_scatter(grad, "narrow", scatter_dimension=0, tiled=True)
    return lax.psum_scatter(grad, "wide", scatter_dimension=1, tiled=True).astype(f32)


def reduce_kernel(count, *refs):
    lefts = refs[:count]
    rights = refs[count : 2 * count]
    vec_ref = refs[2 * count]
    outs = refs[2 * count + 1 : 3 * count + 1]
    vec_out = refs[3 * count + 1]
    rest = refs[3 * count + 2 :]
    per = 12
    bufs = [rest[k * per : (k + 1) * per] for k in range(count)]
    vec_got, vec_sum, send_sem, recv_sem = rest[count * per :]
    x = lax.axis_index("narrow")
    spot = lax.axis_index("wide")
    core = spot % 2
    y = (spot // 2) % 2
    z = spot // 4
    over_x = {"narrow": 1 - x}
    over_y = {"wide": spot + 2 - 4 * y}
    over_core = {"wide": spot + 1 - 2 * core}
    z_of = [z + 1 - 2 * (z % 2), z + 2 - 4 * (z // 2), 3 - z]
    over_z = [{"wide": spot + 4 * (to - z)} for to in z_of]
    partners = [over_x, over_y, over_core] + over_z

    barrier = pltpu.get_barrier_semaphore()
    for partner in partners:
        pl.semaphore_signal(barrier, inc=1, device_id=partner, device_id_type=MESH)
    pl.semaphore_wait(barrier, len(partners))

    used = [0]
    started = []

    def send(source, target, partner):
        k = used[0]
        used[0] += 1
        copy = pltpu.make_async_remote_copy(
            src_ref=source,
            dst_ref=target,
            send_sem=send_sem.at[k],
            recv_sem=recv_sem.at[k],
            device_id=partner,
            device_id_type=MESH,
        )
        copy.start()
        started.append(copy)
        return copy

    from_core = []
    for k in range(count):
        left_pair, right_pair = bufs[k][0], bufs[k][1]
        from_core.append(
            (
                send(lefts[k], left_pair, over_core),
                send(rights[k].at[1 - core], right_pair, over_core),
            )
        )
    steps = [over_core, over_x, over_y, over_z[0], over_z[1]]
    vec_sum[0] = vec_ref[...]
    vec_copy = [send(vec_sum.at[0], vec_got.at[0], steps[0])]

    def vec_step(k):
        vec_copy[-1].wait_recv()
        vec_sum[k + 1] = vec_sum[k] + vec_got[k]
        if k + 1 < len(steps):
            vec_copy.append(send(vec_sum.at[k + 1], vec_got.at[k + 1], steps[k + 1]))

    def unit(k, pair, side, away):
        left_pair, right_pair = bufs[k][0], bufs[k][1]
        rows = right_pair.shape[1] // 2
        own = rights[k][core, side, pair * rows : (pair + 1) * rows, :]
        other = right_pair[side, pair * rows : (pair + 1) * rows, :]
        return jnp.dot(own, lefts[k][away], preferred_element_type=f32) + jnp.dot(
            other, left_pair[away], preferred_element_type=f32
        )

    def phase1(k):
        unused_l, unused_r, sx, sy, rx, ry = bufs[k][:6]

        @pl.loop(0, 2)
        def even(i):
            sx[i] = unit(k, 0, (1 - y) + i * (2 * y - 1), 1).astype(bf16)

        go_x = send(sx, rx, over_x)

        @pl.loop(0, 2)
        def odd(i):
            sy[i] = unit(k, 1, 1 - y, 1 - i).astype(bf16)

        go_y = send(sy, ry, over_y)
        return go_x, go_y

    def phase2(k, waits):
        unused_l, unused_r, sx, sy, rx, ry, ty, tx, r2y, r2x = bufs[k][:10]
        waits[0].wait_recv()
        ty[...] = (unit(k, 0, 1 - y, 0) + rx[0].astype(f32)).astype(bf16)
        go_y = send(ty, r2y, over_y)
        waits[1].wait_recv()
        tx[...] = (unit(k, 1, y, 1) + ry[0].astype(f32)).astype(bf16)
        go_x = send(tx, r2x, over_x)
        return go_y, go_x

    def phase3(k, waits):
        unused_l, unused_r, sx, sy, rx, ry, ty, tx, r2y, r2x, eo, rz = bufs[k]
        block = eo.shape[1]
        waits[0].wait_recv()
        even = unit(k, 0, y, 0) + rx[1].astype(f32) + r2y[...].astype(f32)
        eo[0] = even[:block].astype(bf16)
        eo[1] = even[block:].astype(bf16)
        waits[1].wait_recv()
        odd = unit(k, 1, y, 0) + ry[1].astype(f32) + r2x[...].astype(f32)
        eo[2] = odd[:block].astype(bf16)
        eo[3] = odd[block:].astype(bf16)
        return [send(eo.at[z_of[j]], rz.at[j], over_z[j]) for j in range(3)]

    def phase4(k, waits):
        eo, rz = bufs[k][10], bufs[k][11]
        for copy in waits:
            copy.wait_recv()
        outs[k][...] = (
            eo[z].astype(f32) + rz[0].astype(f32) + rz[1].astype(f32) + rz[2].astype(f32)
        )

    def from_pair(k):
        for copy in from_core[k]:
            copy.wait_recv()

    first, second, third = {}, {}, {}
    from_pair(0)
    first[0] = phase1(0)
    from_pair(1)
    first[1] = phase1(1)
    vec_step(0)
    second[0] = phase2(0, first[0])
    from_pair(3)
    first[3] = phase1(3)
    vec_step(1)
    second[1] = phase2(1, first[1])
    third[0] = phase3(0, second[0])
    from_pair(2)
    first[2] = phase1(2)
    vec_step(2)
    second[3] = phase2(3, first[3])
    third[1] = phase3(1, second[1])
    vec_step(3)
    phase4(0, third[0])
    second[2] = phase2(2, first[2])
    third[3] = phase3(3, second[3])
    phase4(1, third[1])
    third[2] = phase3(2, second[2])
    vec_step(4)
    vec_out[...] = vec_sum[len(steps)]
    phase4(3, third[3])
    phase4(2, third[2])
    for copy in started:
        copy.wait_send()


def reduce_all(links, pairs, vector):
    lefts, rights, outs, scratch = [], [], [], []
    flops = 0
    for left, right in pairs:
        rows, columns = left.shape[1], right.shape[1]
        half, part = rows // 2, columns // 16
        padded = -(-part // 8) * 8
        lefts.append(
            jnp.stack(
                [
                    pick(links.x, left[:, :half], left[:, half:]),
                    pick(links.x, left[:, half:], left[:, :half]),
                ]
            )
        )
        tokens = right.shape[0]
        blocks = right.T.reshape(4, 2, 2, part, tokens).transpose(2, 1, 0, 3, 4)
        blocks = jnp.pad(blocks, ((0, 0), (0, 0), (0, 0), (0, padded - part), (0, 0)))
        rights.append(blocks.reshape(2, 2, 4 * padded, tokens))
        outs.append(jax.ShapeDtypeStruct((padded, half), f32))
        wide = (2 * padded, half)
        scratch += [
            pltpu.VMEM((2, tokens, half), bf16),
            pltpu.VMEM((2, 4 * padded, tokens), bf16),
        ]
        scratch += [pltpu.VMEM((2,) + wide, bf16)] * 4
        scratch += [pltpu.VMEM(wide, bf16)] * 4
        scratch += [pltpu.VMEM((4, padded, half), bf16), pltpu.VMEM((3, padded, half), bf16)]
        flops += 2 * rows * columns * tokens
    count = len(pairs)
    copies = 9 * count + 5
    scratch += [
        pltpu.VMEM((5,) + vector.shape, f32),
        pltpu.VMEM((6,) + vector.shape, f32),
        pltpu.SemaphoreType.DMA((copies,)),
        pltpu.SemaphoreType.DMA((copies,)),
    ]
    outs.append(jax.ShapeDtypeStruct(vector.shape, f32))
    vmem = pl.BlockSpec(memory_space=pltpu.VMEM)
    results = pl.pallas_call(
        functools.partial(reduce_kernel, count),
        out_shape=outs,
        in_specs=[vmem] * (2 * count + 1),
        out_specs=[vmem] * (count + 1),
        scratch_shapes=scratch,
        compiler_params=pltpu.CompilerParams(
            collective_id=1, has_side_effects=True, vmem_limit_bytes=62 * 2**20
        ),
        cost_estimate=pl.CostEstimate(flops=flops, bytes_accessed=30 * 2**20, transcendentals=0),
        name="reduce_grads",
    )(*lefts, *rights, vector)
    grads = []
    for (left, right), out in zip(pairs, results):
        grads.append(out[: right.shape[1] // 16].T)
    return grads, results[-1]


def gather_vectors(links, vectors):
    lengths = [v.shape[0] for v in vectors]
    if not links.direct:
        return [lax.all_gather(v, "narrow", axis=0, tiled=True).astype(f32) for v in vectors]
    packed = jnp.concatenate(vectors)
    other = links.over_x(packed)
    full = []
    at = 0
    for length in lengths:
        mine, theirs = packed[at : at + length], other[at : at + length]
        joined = jnp.concatenate([pick(links.x, mine, theirs), pick(links.x, theirs, mine)])
        full.append(joined.astype(f32))
        at += length
    return full


def all_grads(links, pairs, sums):
    lengths = [v.shape[0] for v in sums]
    width = min(lengths)
    flat = jnp.concatenate(sums)
    if links.direct:
        rows = -(-sum(lengths) // (8 * width)) * 8
        flat = jnp.pad(flat, (0, rows * width - sum(lengths))).reshape(rows, width)
        grads, total = reduce_all(links, pairs, flat)
        total = total.reshape(-1)
    else:
        grads = [generic_grad(links, left, right) for left, right in pairs]
        total = lax.psum(flat, AXES)
    parts = []
    at = 0
    for length in lengths:
        own = length // links.count
        parts.append(lax.dynamic_slice_in_dim(total, at + links.x * own, own, 0))
        at += length
    return grads, parts


def local(
    tokens,
    lengths,
    dropped,
    cotangent,
    first_gain,
    first_shift,
    qkv_weight,
    query_bias,
    value_bias,
    out_weight,
    out_bias,
    second_gain,
    second_shift,
    up_weight,
    up_bias,
    down_weight,
    down_bias,
):
    links = Links()
    rows, width = tokens.shape[1:]
    mask = key_mask(lengths[0], dropped[0], rows)
    inputs = tokens[0].astype(f32)
    grad_out = cotangent[0]
    (gain1, shift1, q_bias, v_bias, o_bias, gain2, shift2, d_bias, u_bias) = gather_vectors(
        links,
        [
            first_gain,
            first_shift,
            query_bias,
            value_bias,
            out_bias,
            second_gain,
            second_shift,
            down_bias,
            up_bias,
        ],
    )
    w_qkv = Weight(links, qkv_weight)
    w_out = Weight(links, out_weight)
    w_up = Weight(links, up_weight)
    w_down = Weight(links, down_weight)

    first = normed(inputs, gain1, shift1).astype(bf16)
    mixed = w_qkv.apply(first)
    query = (mixed[:, :width] + q_bias).astype(bf16)
    keys = mixed[:, width : 2 * width].astype(bf16)
    values = (mixed[:, 2 * width :] + v_bias).astype(bf16)
    attended, logsum = attention(query, keys, values, mask)
    middle = inputs + (w_out.apply(attended) + o_bias)
    second = normed(middle, gain2, shift2).astype(bf16)
    hidden = w_up.apply(second) + u_bias
    active = jax.nn.gelu(hidden, approximate=True).astype(bf16)
    result = middle + (w_down.apply(active) + d_bias)
    output = result.astype(bf16)[None]

    d_active = w_down.apply_t(grad_out)
    unused, gelu_pull = jax.vjp(lambda v: jax.nn.gelu(v, approximate=True), hidden)
    d_hidden = gelu_pull(d_active)[0].astype(bf16)
    d_second = w_up.apply_t(d_hidden)
    unused, norm_pull = jax.vjp(normed, middle, gain2, shift2)
    d_middle, d_gain2, d_shift2 = norm_pull(d_second)
    d_middle = d_middle + grad_out.astype(f32)
    d_branch = d_middle.astype(bf16)
    d_attended = w_out.apply_t(d_branch).astype(bf16)
    d_query, d_keys, d_values = attention_back(query, keys, values, logsum, d_attended, mask)
    d_mixed = jnp.concatenate([d_query, d_keys, d_values], axis=1)
    d_first = w_qkv.apply_t(d_mixed)
    unused, first_pull = jax.vjp(normed, inputs, gain1, shift1)
    d_inputs, d_gain1, d_shift1 = first_pull(d_first)
    grad_tokens = (d_middle + d_inputs)[None]

    def column_sum(values):
        return jnp.sum(values.astype(f32), axis=0)

    grads, vectors = all_grads(
        links,
        [(active, grad_out), (second, d_hidden), (attended, d_branch), (first, d_mixed)],
        [
            d_gain1,
            d_shift1,
            column_sum(d_query),
            column_sum(d_values),
            column_sum(d_branch),
            d_gain2,
            d_shift2,
            column_sum(d_hidden),
            column_sum(grad_out),
        ],
    )
    g_down, g_up, g_out, g_qkv = grads
    v_gain1, v_shift1, v_q, v_v, v_o, v_gain2, v_shift2, v_up, v_down = vectors
    return (
        output,
        grad_tokens,
        v_gain1,
        v_shift1,
        g_qkv,
        v_q,
        v_v,
        g_out,
        v_o,
        v_gain2,
        v_shift2,
        g_up,
        v_up,
        g_down,
        v_down,
    )


def solution(mesh):
    batch = P(AXES, None, None)
    vector = P("narrow")
    matrix = P("narrow", None)
    return jax.shard_map(
        local,
        mesh=mesh,
        in_specs=(
            batch,
            P(AXES),
            P(AXES),
            batch,
            vector,
            vector,
            matrix,
            vector,
            vector,
            matrix,
            vector,
            vector,
            vector,
            matrix,
            vector,
            matrix,
            vector,
        ),
        out_specs=(
            batch,
            batch,
            vector,
            vector,
            P("narrow", "wide"),
            vector,
            vector,
            P("narrow", "wide"),
            vector,
            vector,
            vector,
            P("narrow", "wide"),
            vector,
            P("narrow", "wide"),
            vector,
        ),
        check_vma=False,
    )
```
